32 devices in a mesh: section: 2 (over core), tensor: 4 (over y, x), dp: 4 (over z).
Axes of the slice: x: 2, y: 2, z: 4, core: 2. Of those that a mesh axis runs over, the one named last changes fastest.
Arguments:
- tokens: bfloat16 [512, 4096], P('dp', 'tensor'), may hold values from -6 to 6
- section_weights: bfloat16 [2, 4096, 14336], P('section', None, 'tensor'), may hold values from -0.09375 to 0.09375
- up_weight: bfloat16 [4096, 14336], P(None, 'tensor'), may hold values from -0.09375 to 0.09375
- cotangent: bfloat16 [512, 4096], P('dp'), may hold values from -0.1796875 to 0.1796875
Outputs:
- section_grads: bfloat16 [2, 4096, 14336], P('section', 'dp', 'tensor')
- up_grads: bfloat16 [4096, 14336], P(('section', 'dp'), 'tensor')
The draws below stay inside these ranges and needn't reach their ends.
All inputs are finite; a program needn't handle non-finite values.
Results may differ from the reference program's by a relative error of at most 0.018.
Values may be sent and summed in bfloat16 or wider, within the bound.
No kernel may reach another device: no remote copies, remote signals or barrier semaphores. Data moves between devices by JAX's collectives and lax.ppermute only.
A program may use at most 192 MiB of HBM per device.

```python
import jax
import jax.numpy as jnp
from jax import lax

D = 4096
FFW = 14336
ROWS = 128
TOKENS = 512
N_DP = 4


def level_of(own_key, extent, shards, least, high):
    def one(axis_at, parts):
        steps = jax.random.uniform(jax.random.fold_in(jax.random.fold_in(own_key, 6), axis_at), (parts,), jnp.float32, least / len(shards), high / len(shards))
        return jnp.repeat(jnp.exp(steps), extent[axis_at] // parts).reshape((-1,) + (1,) * (len(extent) - axis_at - 1))

    loudness = one(*shards[0])
    for cut in shards[1:]:
        loudness = loudness * one(*cut)
    return loudness


def normal_values(own_key, extent, spread, reach, pieces=(), kind=jnp.bfloat16):
    factor_of = level_of(own_key, extent, pieces, -0.22, 0.18) if pieces else 1.0
    result = jax.random.normal(own_key, extent, jnp.float32) * spread * factor_of
    return jnp.minimum(jnp.maximum(result, -reach), reach).astype(kind)


def setup_inputs(seed: int = 0) -> dict:
    key_of = jax.random.split(jax.random.key(seed), 5)
    return {
        "tokens": normal_values(key_of[0], (TOKENS, D), 1.0, 6.0, ((0, 4), (1, 4))),
        "section_weights": normal_values(key_of[1], (2, D, FFW), D ** -0.5, 0.09375, ((0, 2), (2, 4))),
        "up_weight": normal_values(key_of[2], (D, FFW), D ** -0.5, 0.09375, ((1, 4),)),
        "cotangent": normal_values(key_of[3], (TOKENS, D), 0.03, 0.1796875, ((0, 4),)),
    }


def along_rows(left, right):
    return lax.dot_general(left, right, (((0,), (0,)), ((), ())), preferred_element_type=jnp.float32)


def reference(tokens, section_weights, up_weight, cotangent):
    gate_weight = section_weights[0]
    down_trans = section_weights[1]
    token_groups = tokens.reshape(N_DP, ROWS, D)
    incoming_groups = cotangent.reshape(N_DP, ROWS, D)

    def group_step(carry, pair):
        token_rows, incoming = pair
        gate_pre = jnp.dot(token_rows, gate_weight, preferred_element_type=jnp.float32)
        up_pre = jnp.dot(token_rows, up_weight, preferred_element_type=jnp.float32)
        sigmoid_gate = jax.nn.sigmoid(gate_pre)
        hidden = (gate_pre * sigmoid_gate * up_pre).astype(jnp.bfloat16)
        grad_hidden = jnp.dot(incoming, down_trans, preferred_element_type=jnp.float32)
        grad_gate = (grad_hidden * up_pre * sigmoid_gate * (1.0 + gate_pre * (1.0 - sigmoid_gate))).astype(jnp.bfloat16)
        grad_up = (grad_hidden * gate_pre * sigmoid_gate).astype(jnp.bfloat16)
        gate_part = along_rows(token_rows, grad_gate).astype(jnp.bfloat16)
        down_part = along_rows(incoming, hidden).astype(jnp.bfloat16)
        up_part = along_rows(token_rows, grad_up).astype(jnp.bfloat16)
        gate_part, down_part, up_part = lax.optimization_barrier((gate_part, down_part, up_part))
        gate_sum, down_sum, up_sum = carry
        return (gate_sum + gate_part.astype(jnp.float32), down_sum + down_part.astype(jnp.float32), up_sum + up_part.astype(jnp.float32)), None

    zeros = jnp.zeros((D, FFW), jnp.float32)
    (gate_sum, down_sum, up_sum), _ = lax.scan(group_step, (zeros, zeros, zeros), (token_groups, incoming_groups))
    return jnp.stack([gate_sum, down_sum]).astype(jnp.bfloat16), up_sum.astype(jnp.bfloat16)
```

```python
import jax
import jax.numpy as jnp
from jax import lax
from jax.sharding import PartitionSpec as P

AXES = ("section", "tensor", "dp")


def sent(value, mesh, target):
    shape = [mesh.shape[axis] for axis in AXES]
    pairs = []
    for s in range(shape[0]):
        for t in range(shape[1]):
            for d in range(shape[2]):
                source = (s * shape[1] + t) * shape[2] + d
                to = target(s, t, d)
                pairs.append((source, (to[0] * shape[1] + to[1]) * shape[2] + to[2]))
    return lax.ppermute(value, AXES, pairs)


def matmul(left, right):
    return jnp.dot(left, right, preferred_element_type=jnp.float32)


def along_rows(left, right):
    return lax.dot_general(
        left, right, (((0,), (0,)), ((), ())), preferred_element_type=jnp.float32
    )


def columns(value, start, width):
    return lax.dynamic_slice_in_dim(value, start, width, 1)


def placed_at(whole, piece, row, column):
    return lax.dynamic_update_slice(whole, piece, (row, column))


def gathered_everywhere(tokens, cotangent):
    tokens_all = lax.all_gather(tokens, "tensor", axis=1, tiled=True)
    tokens_all = lax.all_gather(tokens_all, "dp", axis=0, tiled=True)
    return tokens_all, lax.all_gather(cotangent, "dp", axis=0, tiled=True)


def gathered_by_chip(mesh, tokens, cotangent):
    groups = mesh.shape["dp"]
    section = lax.axis_index("section")
    tensor = lax.axis_index("tensor")
    count, block = tokens.shape
    half = block // 2
    width = cotangent.shape[1]
    quarter = width // 4

    def ring(step):
        return lambda s, t, d: (s, t, (d + step) % groups)

    def other_section(s, t, d):
        return (1 - s, t, d)

    def near(s, t, d):
        return (s, t ^ (1 + s), d)

    def far(s, t, d):
        return (s, t ^ (2 - s), d)

    steps = range(1, groups)
    parity = (tensor ^ (tensor >> 1)) & 1
    own_half = columns(tokens, section * half, half)
    mine = jnp.concatenate([own_half] + [sent(own_half, mesh, ring(k)) for k in steps], 0)
    own_quarter = columns(cotangent, (2 * parity + section) * quarter, quarter)
    first_mine = jnp.concatenate([sent(own_quarter, mesh, ring(k)) for k in steps], 0)
    theirs = sent(mine, mesh, other_section)
    both = jnp.concatenate([mine, theirs], 1)
    beside = sent(both, mesh, near)
    beside_too = sent(beside, mesh, other_section)
    across = sent(beside[:, :half], mesh, far)
    across_too = sent(across, mesh, other_section)
    first_theirs = sent(first_mine, mesh, other_section)
    second_mine = sent(first_mine, mesh, near)
    second_theirs = sent(second_mine, mesh, other_section)

    tokens_all = jnp.zeros((count * groups, width), tokens.dtype)
    near_block = tensor ^ (1 + section)
    far_block = tensor ^ (2 - section)
    for piece, at in (
        (mine, 2 * tensor + section),
        (theirs, 2 * tensor + 1 - section),
        (beside[:, :half], 2 * near_block + section),
        (beside[:, half:], 2 * near_block + 1 - section),
        (beside_too[:, :half], 2 * far_block + 1 - section),
        (beside_too[:, half:], 2 * far_block + section),
        (across, 2 * (tensor ^ 3) + section),
        (across_too, 2 * (tensor ^ 3) + 1 - section),
    ):
        tokens_all = placed_at(tokens_all, piece, 0, at * half)
    cotangent_all = jnp.zeros((count * groups, width), cotangent.dtype)
    cotangent_all = placed_at(cotangent_all, cotangent, 0, 0)
    for piece, at in (
        (first_mine, 2 * parity + section),
        (first_theirs, 2 * parity + 1 - section),
        (second_mine, 2 * (1 - parity) + section),
        (second_theirs, 2 * (1 - parity) + 1 - section),
    ):
        cotangent_all = placed_at(cotangent_all, piece, count, at * quarter)
    return tokens_all, cotangent_all


def local(mesh, tokens, section_weights, up_weight, cotangent):
    section = lax.axis_index("section")
    group = lax.axis_index("dp")
    groups = mesh.shape["dp"]
    is_first = section == 0
    slot = section_weights[0]
    units = slot.shape[1]
    width = cotangent.shape[1]

    def swapped(value):
        return sent(value, mesh, lambda s, t, d: (1 - s, t, d))

    if mesh.shape["tensor"] == 4:
        tokens_all, cotangent_all = gathered_by_chip(mesh, tokens, cotangent)
    else:
        tokens_all, cotangent_all = gathered_everywhere(tokens, cotangent)

    used = jnp.where(is_first, tokens_all, cotangent_all)
    own = matmul(used, slot).astype(jnp.bfloat16)
    other = swapped(own)
    half = units // 2
    up_own = matmul(tokens_all, columns(up_weight, section * half, half)).astype(jnp.bfloat16)
    up_other = swapped(up_own)
    up_pre = jnp.where(
        is_first,
        jnp.concatenate([up_own, up_other], 1),
        jnp.concatenate([up_other, up_own], 1),
    ).astype(jnp.float32)
    gate_pre = jnp.where(is_first, own, other).astype(jnp.float32)
    grad_hidden = jnp.where(is_first, other, own).astype(jnp.float32)
    sigmoid_gate = jax.nn.sigmoid(gate_pre)
    silu = gate_pre * sigmoid_gate
    grad_up = (grad_hidden * silu).astype(jnp.bfloat16)
    grad_gate = grad_hidden * up_pre * sigmoid_gate * (1.0 + gate_pre * (1.0 - sigmoid_gate))
    right = jnp.where(is_first, grad_gate, silu * up_pre).astype(jnp.bfloat16)
    slot_rows = width // groups
    up_rows = slot_rows // 2
    slot_sum = along_rows(columns(used, group * slot_rows, slot_rows), right)
    up_sum = along_rows(columns(tokens_all, (section * groups + group) * up_rows, up_rows), grad_up)
    return (slot_sum.astype(jnp.bfloat16)[None], up_sum.astype(jnp.bfloat16))


def solution(mesh):
    placed = (P("dp", "tensor"), P("section", None, "tensor"), P(None, "tensor"), P("dp", None))
    return jax.shard_map(
        lambda *args: local(mesh, *args),
        mesh=mesh,
        in_specs=placed,
        out_specs=(P("section", "dp", "tensor"), P(("section", "dp"), "tensor")),
        check_vma=False,
    )
```

```python
import jax
import jax.numpy as jnp
from jax import lax
from jax.experimental import pallas as pl
from jax.experimental.pallas import tpu as pltpu
from jax.sharding import PartitionSpec as P


AXES = ("section", "tensor", "dp")
TILE = 512


def sent(value, mesh, target):
    shape = [mesh.shape[axis] for axis in AXES]
    pairs = []
    for s in range(shape[0]):
        for t in range(shape[1]):
            for d in range(shape[2]):
                source = (s * shape[1] + t) * shape[2] + d
                to = target(s, t, d)
                pairs.append((source, (to[0] * shape[1] + to[1]) * shape[2] + to[2]))
    return lax.ppermute(value, AXES, pairs)


def matmul(left, right):
    return jnp.dot(left, right, preferred_element_type=jnp.float32)


def along_rows(left, right):
    return lax.dot_general(
        left, right, (((0,), (0,)), ((), ())), preferred_element_type=jnp.float32
    )


def columns(value, start, width):
    return lax.dynamic_slice_in_dim(value, start, width, 1)


def gradients(gate_pre, up_pre, grad_hidden, is_first):
    sigmoid_gate = jax.nn.sigmoid(gate_pre)
    silu = gate_pre * sigmoid_gate
    grad_gate = grad_hidden * up_pre * sigmoid_gate * (1.0 + gate_pre * (1.0 - sigmoid_gate))
    right = jnp.where(is_first, grad_gate, silu * up_pre)
    return right.astype(jnp.bfloat16), (grad_hidden * silu).astype(jnp.bfloat16)


def local_plain(mesh, tokens, section_weights, up_weight, cotangent):
    section = lax.axis_index("section")
    group = lax.axis_index("dp")
    groups = mesh.shape["dp"]
    is_first = section == 0
    slot = section_weights[0]
    units = slot.shape[1]
    width = cotangent.shape[1]

    def swapped(value):
        return sent(value, mesh, lambda s, t, d: (1 - s, t, d))

    tokens_all = lax.all_gather(tokens, "tensor", axis=1, tiled=True)
    tokens_all = lax.all_gather(tokens_all, "dp", axis=0, tiled=True)
    cotangent_all = lax.all_gather(cotangent, "dp", axis=0, tiled=True)
    used = jnp.where(is_first, tokens_all, cotangent_all)
    own = matmul(used, slot).astype(jnp.bfloat16)
    other = swapped(own)
    half = units // 2
    up_own = matmul(tokens_all, columns(up_weight, section * half, half)).astype(jnp.bfloat16)
    up_other = swapped(up_own)
    up_pre = jnp.where(
        is_first,
        jnp.concatenate([up_own, up_other], 1),
        jnp.concatenate([up_other, up_own], 1),
    ).astype(jnp.float32)
    gate_pre = jnp.where(is_first, own, other).astype(jnp.float32)
    grad_hidden = jnp.where(is_first, other, own).astype(jnp.float32)
    right, grad_up = gradients(gate_pre, up_pre, grad_hidden, is_first)
    slot_rows = width // groups
    up_rows = slot_rows // 2
    slot_sum = along_rows(columns(used, group * slot_rows, slot_rows), right)
    up_sum = along_rows(columns(tokens_all, (section * groups + group) * up_rows, up_rows), grad_up)
    return (slot_sum.astype(jnp.bfloat16)[None], up_sum.astype(jnp.bfloat16))


def cost(flops, moved):
    return pl.CostEstimate(flops=int(flops), bytes_accessed=int(moved), transcendentals=0)


def product(info, pieces, weight, first_tile, tiles, dtype, start=None, head=None, room=None):
    arrays = []
    for array, _, _, _ in pieces:
        if not any(array is a for a in arrays):
            arrays.append(array)
    which = [next(i for i, a in enumerate(arrays) if a is array) for array, _, _, _ in pieces]
    count = arrays[0].shape[0]
    above = 0 if head is None else head.shape[0]

    def kernel(info_ref, *refs):
        lefts = refs[: len(arrays)]
        rights = refs[len(arrays) : len(arrays) + len(pieces)]
        rest = list(refs[len(arrays) + len(pieces) :])
        out = rest.pop()
        total = None
        for (_, begin, depth, _), i, right in zip(pieces, which, rights):
            term = matmul(lefts[i][:, begin : begin + depth], right[...])
            total = term if total is None else total + term
        if start is not None:
            total = total + rest.pop(0)[...].astype(jnp.float32)
        if head is not None:
            out[:above, :] = rest.pop(0)[...]
        out[above:, :] = total.astype(dtype)

    specs = [pl.BlockSpec(a.shape, lambda j, info: (0, 0)) for a in arrays]
    for _, _, depth, row in pieces:
        specs.append(
            pl.BlockSpec((depth, TILE), lambda j, info, row=row: (row(info), first_tile + j))
        )
    operands = list(arrays) + [weight] * len(pieces)
    for extra in (start, head):
        if extra is not None:
            specs.append(pl.BlockSpec((extra.shape[0], TILE), lambda j, info: (0, first_tile + j)))
            operands.append(extra)
    out = jax.ShapeDtypeStruct((above + count, (room or tiles) * TILE), dtype)
    deep = sum(p[2] for p in pieces)
    return pl.pallas_call(
        kernel,
        grid_spec=pltpu.PrefetchScalarGridSpec(
            num_scalar_prefetch=1,
            grid=(tiles,),
            in_specs=specs,
            out_specs=pl.BlockSpec((above + count, TILE), lambda j, info: (0, j)),
        ),
        out_shape=out,
        compiler_params=pltpu.CompilerParams(vmem_limit_bytes=48 * 1024 * 1024),
        cost_estimate=cost(2 * count * deep * tiles * TILE, 2 * deep * tiles * TILE + out.size * 2),
    )(info, *operands)


def unset(shape, dtype):
    return pl.pallas_call(
        lambda out: None,
        out_shape=jax.ShapeDtypeStruct(shape, dtype),
        out_specs=pl.BlockSpec(memory_space=pl.ANY),
    )()


def outputs(is_gate, left_slot, left_up, gate, hidden, ups, up_of, first, units, begun):
    tiles = gate.shape[1] // TILE
    count = gate.shape[0]
    used = sorted({up_of(first + j)[0] for j in range(tiles)})

    def kernel(a_slot, a_up, gate_ref, hidden_ref, *refs):
        up_refs = refs[: len(used)]
        slot_ref, up_ref = refs[-2:]
        gate_pre = gate_ref[...].astype(jnp.float32)
        grad_hidden = hidden_ref[...].astype(jnp.float32)
        up_pre = up_refs[0][...]
        if len(used) == 2:
            j = pl.program_id(0) + first
            early = sum(up_of(first + k)[0] == used[0] for k in range(tiles)) + first
            up_pre = jnp.where(j < early, up_pre, up_refs[1][...])
        up_pre = up_pre.astype(jnp.float32)
        sigmoid_gate = jax.nn.sigmoid(gate_pre)
        silu = gate_pre * sigmoid_gate
        grad_up = (grad_hidden * silu).astype(jnp.bfloat16)
        if is_gate:
            right = grad_hidden * up_pre * sigmoid_gate * (1.0 + gate_pre * (1.0 - sigmoid_gate))
        else:
            right = silu * up_pre
        slot_ref[...] = along_rows(a_slot[...], right.astype(jnp.bfloat16)).astype(jnp.bfloat16)
        up_ref[...] = along_rows(a_up[...], grad_up).astype(jnp.bfloat16)

    def up_tile(which):
        own = [k for k in range(tiles) if up_of(first + k)[0] == which]
        base = up_of(first + own[0])[1] - own[0]
        return lambda j: (0, jnp.clip(j, own[0], own[-1]) + base)

    whole = lambda j: (0, 0)
    here = lambda j: (0, j)
    there = lambda j: (0, j + first)
    block = (count, TILE)
    specs = [
        pl.BlockSpec(left_slot.shape, whole),
        pl.BlockSpec(left_up.shape, whole),
        pl.BlockSpec(block, here),
        pl.BlockSpec(block, here),
    ] + [pl.BlockSpec(block, up_tile(k)) for k in used]
    operands = [left_slot, left_up, gate, hidden] + [ups[k] for k in used]
    rows = (left_slot.shape[1], left_up.shape[1])
    aliases = {}
    if begun is not None:
        specs += [pl.BlockSpec(memory_space=pl.ANY)] * 2
        aliases = {len(operands): 0, 1 + len(operands): 1}
        operands += list(begun)
    return pl.pallas_call(
        kernel,
        grid=(tiles,),
        in_specs=specs,
        out_specs=[pl.BlockSpec((r, TILE), there) for r in rows],
        out_shape=[jax.ShapeDtypeStruct((r, units), jnp.bfloat16) for r in rows],
        input_output_aliases=aliases,
        compiler_params=pltpu.CompilerParams(vmem_limit_bytes=48 * 1024 * 1024),
        cost_estimate=cost(
            2 * count * sum(rows) * tiles * TILE, 2 * tiles * TILE * (4 * count + sum(rows))
        ),
    )(*operands)


def local_by_chip(mesh, tokens, section_weights, up_weight, cotangent):
    groups = mesh.shape["dp"]
    section = lax.axis_index("section")
    tensor = lax.axis_index("tensor")
    group = lax.axis_index("dp")
    is_first = section == 0
    place = lax.broadcasted_iota(jnp.int32, (3,), 0)
    info = jnp.where(place == 0, section, jnp.where(place == 1, tensor, group)).astype(jnp.int32)
    slot = section_weights[0]
    count, block = tokens.shape
    half = block // 2
    width, units = slot.shape
    quarter = width // 4
    everyone = groups * count
    tiles = units // TILE
    most = (tiles + 1) // 2
    few = tiles - most
    low = jnp.bfloat16

    def moved(value, target):
        return sent(value, mesh, target)

    def ring(step):
        return lambda s, t, d: (s, t, (d + step) % groups)

    def other_section(s, t, d):
        return (1 - s, t, d)

    def near(s, t, d):
        return (s, t ^ (1 + s), d)

    def far(s, t, d):
        return (s, t ^ (2 - s), d)

    steps = range(1, groups)
    parity = (tensor ^ (tensor >> 1)) & 1
    own_half = columns(tokens, section * half, half)
    own_quarter = columns(cotangent, (2 * parity + section) * quarter, quarter)

    mine = jnp.concatenate([own_half] + [moved(own_half, ring(k)) for k in steps], 0)
    theirs = moved(mine, other_section)
    first_mine = jnp.concatenate([moved(own_quarter, ring(k)) for k in steps], 0)
    both = jnp.concatenate([mine, theirs], 1)
    beside = moved(both, near)
    beside_too = moved(beside, other_section)
    across = moved(beside[:, :half], far)
    across_too = moved(across, other_section)
    first_theirs = moved(first_mine, other_section)
    second_mine = moved(first_mine, near)
    second_theirs = moved(second_mine, other_section)

    def odd(i):
        return (i[1] ^ (i[1] >> 1)) & 1

    here = [
        (both, 0, half, lambda i: 2 * i[1] + i[0]),
        (both, half, half, lambda i: 2 * i[1] + 1 - i[0]),
    ]
    rest = [
        (beside, 0, half, lambda i: 2 * (i[1] ^ (1 + i[0])) + i[0]),
        (beside, half, half, lambda i: 2 * (i[1] ^ (1 + i[0])) + 1 - i[0]),
        (beside_too, 0, half, lambda i: 2 * (i[1] ^ (2 - i[0])) + 1 - i[0]),
        (beside_too, half, half, lambda i: 2 * (i[1] ^ (2 - i[0])) + i[0]),
        (across, 0, half, lambda i: 2 * (i[1] ^ 3) + i[0]),
        (across_too, 0, half, lambda i: 2 * (i[1] ^ 3) + 1 - i[0]),
    ]
    cots = [
        (first_mine, 0, quarter, lambda i: 2 * odd(i) + i[0]),
        (first_theirs, 0, quarter, lambda i: 2 * odd(i) + 1 - i[0]),
        (second_mine, 0, quarter, lambda i: 2 * (1 - odd(i)) + i[0]),
        (second_theirs, 0, quarter, lambda i: 2 * (1 - odd(i)) + 1 - i[0]),
    ]
    whole = [(cotangent, 0, width, lambda i: 0)]

    begun, own_rows = lax.cond(
        is_first,
        lambda: (
            product(info, here, slot, 0, tiles, jnp.float32),
            unset((count, units), low),
        ),
        lambda: (unset((everyone, units), jnp.float32), product(info, whole, slot, 0, tiles, low)),
    )
    one = lax.cond(
        is_first,
        lambda: product(info, rest, slot, 0, most, low, start=begun),
        lambda: product(info, here + rest, up_weight, few, most, low),
    )
    one_passed = moved(one, other_section)
    two = lax.cond(
        is_first,
        lambda: product(info, here + rest, up_weight, 0, few, low, room=most),
        lambda: product(info, cots, slot, 0, most, low, head=own_rows),
    )
    two_passed = moved(two, other_section)
    three = lax.cond(
        is_first,
        lambda: product(info, rest, slot, most, few, low, start=begun),
        lambda: product(info, cots, slot, most, few, low, head=own_rows),
    )
    three_passed = moved(three, other_section)

    def token_columns(at):
        chosen = None
        for array, begin, depth, row in here + rest:
            piece = array[:, begin : begin + depth]
            hit = row((section, tensor, group)) == at
            chosen = piece if chosen is None else jnp.where(hit, piece, chosen)
        return chosen

    def cotangent_columns(at):
        chosen = None
        for array, _, _, row in cots:
            hit = row((section, tensor, group)) == at
            chosen = array if chosen is None else jnp.where(hit, array, chosen)
        return jnp.concatenate([columns(cotangent, at * quarter, quarter), chosen], 0)

    left_slot, left_up = lax.cond(
        is_first,
        lambda: (
            jnp.concatenate([token_columns(2 * group), token_columns(2 * group + 1)], 1),
            token_columns(group),
        ),
        lambda: (cotangent_columns(group), token_columns(groups + group)),
    )

    def up_of(j):
        return (0, j) if j < few else (1, j - few)

    grads = lax.cond(
        is_first,
        lambda: outputs(
            True, left_slot, left_up, one, two_passed, (two, one_passed), up_of, 0, units, None
        ),
        lambda: outputs(
            False, left_slot, left_up, one_passed, two, (two_passed, one), up_of, 0, units, None
        ),
    )
    slot_sum, up_sum = lax.cond(
        is_first,
        lambda: outputs(
            True, left_slot, left_up, three, three_passed, (two, one_passed), up_of, most,
            units, grads,
        ),
        lambda: outputs(
            False, left_slot, left_up, three_passed, three, (two_passed, one), up_of, most,
            units, grads,
        ),
    )
    return (slot_sum[None], up_sum)


def solution(mesh):
    placed = (P("dp", "tensor"), P("section", None, "tensor"), P(None, "tensor"), P("dp", None))
    by_chip = mesh.shape["tensor"] == 4 and mesh.shape["dp"] == 4 and mesh.shape["section"] == 2

    def body(*arrays):
        return (local_by_chip if by_chip else local_plain)(mesh, *arrays)

    return jax.shard_map(
        body,
        mesh=mesh,
        in_specs=placed,
        out_specs=(P("section", "dp", "tensor"), P(("section", "dp"), "tensor")),
        check_vma=False,
    )
```

```python
import jax
import jax.numpy as jnp
from jax import lax
from jax.experimental import pallas as pl
from jax.experimental.pallas import tpu as pltpu
from jax.sharding import PartitionSpec as P


AXES = ("section", "tensor", "dp")
TILE = 512


def sent(value, mesh, target):
    shape = [mesh.shape[axis] for axis in AXES]
    pairs = []
    for s in range(shape[0]):
        for t in range(shape[1]):
            for d in range(shape[2]):
                source = (s * shape[1] + t) * shape[2] + d
                to = target(s, t, d)
                pairs.append((source, (to[0] * shape[1] + to[1]) * shape[2] + to[2]))
    return lax.ppermute(value, AXES, pairs)


def matmul(left, right):
    return jnp.dot(left, right, preferred_element_type=jnp.float32)


def along_rows(left, right):
    return lax.dot_general(
        left, right, (((0,), (0,)), ((), ())), preferred_element_type=jnp.float32
    )


def columns(value, start, width):
    return lax.dynamic_slice_in_dim(value, start, width, 1)


def gradients(gate_pre, up_pre, grad_hidden, is_first):
    sigmoid_gate = jax.nn.sigmoid(gate_pre)
    silu = gate_pre * sigmoid_gate
    grad_gate = grad_hidden * up_pre * sigmoid_gate * (1.0 + gate_pre * (1.0 - sigmoid_gate))
    right = jnp.where(is_first, grad_gate, silu * up_pre)
    return right.astype(jnp.bfloat16), (grad_hidden * silu).astype(jnp.bfloat16)


def local_plain(mesh, tokens, section_weights, up_weight, cotangent):
    section = lax.axis_index("section")
    group = lax.axis_index("dp")
    groups = mesh.shape["dp"]
    is_first = section == 0
    slot = section_weights[0]
    units = slot.shape[1]
    width = cotangent.shape[1]

    def swapped(value):
        return sent(value, mesh, lambda s, t, d: (1 - s, t, d))

    tokens_all = lax.all_gather(tokens, "tensor", axis=1, tiled=True)
    tokens_all = lax.all_gather(tokens_all, "dp", axis=0, tiled=True)
    cotangent_all = lax.all_gather(cotangent, "dp", axis=0, tiled=True)
    used = jnp.where(is_first, tokens_all, cotangent_all)
    own = matmul(used, slot).astype(jnp.bfloat16)
    other = swapped(own)
    half = units // 2
    up_own = matmul(tokens_all, columns(up_weight, section * half, half)).astype(jnp.bfloat16)
    up_other = swapped(up_own)
    up_pre = jnp.where(
        is_first,
        jnp.concatenate([up_own, up_other], 1),
        jnp.concatenate([up_other, up_own], 1),
    ).astype(jnp.float32)
    gate_pre = jnp.where(is_first, own, other).astype(jnp.float32)
    grad_hidden = jnp.where(is_first, other, own).astype(jnp.float32)
    right, grad_up = gradients(gate_pre, up_pre, grad_hidden, is_first)
    slot_rows = width // groups
    up_rows = slot_rows // 2
    slot_sum = along_rows(columns(used, group * slot_rows, slot_rows), right)
    up_sum = along_rows(columns(tokens_all, (section * groups + group) * up_rows, up_rows), grad_up)
    return (slot_sum.astype(jnp.bfloat16)[None], up_sum.astype(jnp.bfloat16))


def cost(flops, moved):
    return pl.CostEstimate(flops=int(flops), bytes_accessed=int(moved), transcendentals=0)


def product(info, pieces, weight, first_tile, tiles, dtype, start=None, head=None, room=None):
    arrays = []
    for array, _, _, _ in pieces:
        if not any(array is a for a in arrays):
            arrays.append(array)
    which = [next(i for i, a in enumerate(arrays) if a is array) for array, _, _, _ in pieces]
    count = arrays[0].shape[0]
    above = 0 if head is None else head.shape[0]

    def kernel(info_ref, *refs):
        lefts = refs[: len(arrays)]
        rights = refs[len(arrays) : len(arrays) + len(pieces)]
        rest = list(refs[len(arrays) + len(pieces) :])
        out = rest.pop()
        total = None
        for (_, begin, depth, _), i, right in zip(pieces, which, rights):
            term = matmul(lefts[i][:, begin : begin + depth], right[...])
            total = term if total is None else total + term
        if start is not None:
            total = total + rest.pop(0)[...].astype(jnp.float32)
        if head is not None:
            out[:above, :] = rest.pop(0)[...]
        out[above:, :] = total.astype(dtype)

    specs = [pl.BlockSpec(a.shape, lambda j, info: (0, 0)) for a in arrays]
    for _, _, depth, row in pieces:
        specs.append(
            pl.BlockSpec((depth, TILE), lambda j, info, row=row: (row(info), first_tile + j))
        )
    operands = list(arrays) + [weight] * len(pieces)
    for extra in (start, head):
        if extra is not None:
            specs.append(pl.BlockSpec((extra.shape[0], TILE), lambda j, info: (0, first_tile + j)))
            operands.append(extra)
    out = jax.ShapeDtypeStruct((above + count, (room or tiles) * TILE), dtype)
    deep = sum(p[2] for p in pieces)
    return pl.pallas_call(
        kernel,
        grid_spec=pltpu.PrefetchScalarGridSpec(
            num_scalar_prefetch=1,
            grid=(tiles,),
            in_specs=specs,
            out_specs=pl.BlockSpec((above + count, TILE), lambda j, info: (0, j)),
        ),
        out_shape=out,
        compiler_params=pltpu.CompilerParams(vmem_limit_bytes=48 * 1024 * 1024),
        cost_estimate=cost(2 * count * deep * tiles * TILE, 2 * deep * tiles * TILE + out.size * 2),
    )(info, *operands)


def unset(shape, dtype):
    return pl.pallas_call(
        lambda out: None,
        out_shape=jax.ShapeDtypeStruct(shape, dtype),
        out_specs=pl.BlockSpec(memory_space=pl.ANY),
    )()


def picked(info, blocks):
    def kernel(info_ref, *refs):
        for source, out in zip(refs[: len(blocks)], refs[len(blocks) :]):
            out[...] = source[...]

    shapes = [(array.shape[0], wide) for array, wide, _ in blocks]
    return pl.pallas_call(
        kernel,
        grid_spec=pltpu.PrefetchScalarGridSpec(
            num_scalar_prefetch=1,
            grid=(1,),
            in_specs=[
                pl.BlockSpec(shape, lambda j, info, which=which: (0, which(info)))
                for shape, (_, _, which) in zip(shapes, blocks)
            ],
            out_specs=[pl.BlockSpec(shape, lambda j, info: (0, 0)) for shape in shapes],
        ),
        out_shape=[
            jax.ShapeDtypeStruct(shape, array.dtype) for shape, (array, _, _) in zip(shapes, blocks)
        ],
    )(info, *[array for array, _, _ in blocks])


def stacked(arrays):
    count, wide = arrays[0].shape

    def kernel(*refs):
        for k, source in enumerate(refs[:-1]):
            refs[-1][k * count : (k + 1) * count, :] = source[...]

    return pl.pallas_call(
        kernel,
        out_shape=jax.ShapeDtypeStruct((len(arrays) * count, wide), arrays[0].dtype),
    )(*arrays)


def outputs(info, is_gate, slot_parts, up_parts, gate, hidden, up_pre, first, units, begun):
    tiles = gate.shape[1] // TILE
    count = gate.shape[0]
    parts = slot_parts + up_parts
    sources = []
    for _, _, options in parts:
        for _, array, _ in options:
            if not any(array is known for known in sources):
                sources.append(array)

    def kernel(info_ref, gate_ref, hidden_ref, up_pre_ref, *refs):
        held = refs[: len(sources)]
        slot_ref, up_ref, left_slot, left_up, arrived = refs[-5:]

        def copies():
            for n, (rows, cols, options) in enumerate(parts):
                target = (left_slot if n < len(slot_parts) else left_up).at[rows, cols]
                for when, array, taken in options:
                    ref = next(r for r, known in zip(held, sources) if known is array)
                    source = ref.at[:, taken(info_ref)]
                    yield n, when, pltpu.make_async_copy(source, target, arrived.at[n])

        @pl.when(pl.program_id(0) == 0)
        def _():
            for _, when, copy in copies():
                pl.when(when(info_ref))(copy.start)
            for _, when, copy in copies():
                pl.when(when(info_ref))(copy.wait)

        gate_pre = gate_ref[...].astype(jnp.float32)
        grad_hidden = hidden_ref[...].astype(jnp.float32)
        up_pre = up_pre_ref[...].astype(jnp.float32)
        sigmoid_gate = jax.nn.sigmoid(gate_pre)
        silu = gate_pre * sigmoid_gate
        grad_up = (grad_hidden * silu).astype(jnp.bfloat16)
        if is_gate:
            right = grad_hidden * up_pre * sigmoid_gate * (1.0 + gate_pre * (1.0 - sigmoid_gate))
        else:
            right = silu * up_pre
        right = right.astype(jnp.bfloat16)

        slot_ref[...] = along_rows(left_slot[...], right).astype(jnp.bfloat16)
        up_ref[...] = along_rows(left_up[...], grad_up).astype(jnp.bfloat16)

    here = lambda j, info: (0, j)
    there = lambda j, info: (0, j + first)
    block = (count, TILE)
    specs = [pl.BlockSpec(block, here)] * 3 + [pl.BlockSpec(memory_space=pl.ANY)] * len(sources)
    operands = [gate, hidden, up_pre] + sources
    slot_rows = max(part[1].stop for part in slot_parts)
    up_rows = max(part[1].stop for part in up_parts)
    rows = (slot_rows, up_rows)
    aliases = {}
    if begun is not None:
        specs += [pl.BlockSpec(memory_space=pl.ANY)] * 2
        aliases = {1 + len(operands): 0, 2 + len(operands): 1}
        operands += list(begun)
    return pl.pallas_call(
        kernel,
        grid_spec=pltpu.PrefetchScalarGridSpec(
            num_scalar_prefetch=1,
            grid=(tiles,),
            in_specs=specs,
            out_specs=[pl.BlockSpec((r, TILE), there) for r in rows],
            scratch_shapes=[pltpu.VMEM((count, r), jnp.bfloat16) for r in rows]
            + [pltpu.SemaphoreType.DMA((len(parts),))],
        ),
        out_shape=[jax.ShapeDtypeStruct((r, units), jnp.bfloat16) for r in rows],
        input_output_aliases=aliases,
        compiler_params=pltpu.CompilerParams(vmem_limit_bytes=48 * 1024 * 1024),
        cost_estimate=cost(
            2 * count * sum(rows) * tiles * TILE, 2 * tiles * TILE * (3 * count + sum(rows))
        ),
    )(info, *operands)


def local_by_chip(mesh, tokens, section_weights, up_weight, cotangent):
    groups = mesh.shape["dp"]
    section = lax.axis_index("section")
    tensor = lax.axis_index("tensor")
    group = lax.axis_index("dp")
    is_first = section == 0
    place = lax.broadcasted_iota(jnp.int32, (3,), 0)
    info = jnp.where(place == 0, section, jnp.where(place == 1, tensor, group)).astype(jnp.int32)
    slot = section_weights[0]
    count, block = tokens.shape
    half = block // 2
    width, units = slot.shape
    quarter = width // 4
    everyone = groups * count
    tiles = units // TILE
    most = (tiles + 1) // 2
    few = tiles - most
    low = jnp.bfloat16

    def moved(value, target):
        return sent(value, mesh, target)

    def ring(step):
        return lambda s, t, d: (s, t, (d + step) % groups)

    def other_section(s, t, d):
        return (1 - s, t, d)

    def near(s, t, d):
        return (s, t ^ (1 + s), d)

    def far(s, t, d):
        return (s, t ^ (2 - s), d)

    steps = range(1, groups)

    def odd(i):
        return (i[1] ^ (i[1] >> 1)) & 1

    (own_half,) = picked(info, [(tokens, half, lambda i: i[0])])
    parity = (tensor ^ (tensor >> 1)) & 1
    own_quarter = columns(cotangent, (2 * parity + section) * quarter, quarter)

    mine = jnp.concatenate([own_half] + [moved(own_half, ring(k)) for k in steps], 0)
    theirs = moved(mine, other_section)
    first_mine = stacked([moved(own_quarter, ring(k)) for k in steps])
    beside = moved(mine, near)
    beside_too = moved(beside, other_section)
    below = moved(mine, far)
    below_too = moved(below, other_section)
    across = moved(beside, far)
    across_too = moved(across, other_section)
    first_theirs = moved(first_mine, other_section)
    second_mine = moved(first_mine, near)
    second_theirs = moved(second_mine, other_section)

    here = [
        (mine, 0, half, lambda i: 2 * i[1] + i[0]),
        (theirs, 0, half, lambda i: 2 * i[1] + 1 - i[0]),
    ]
    rest = [
        (beside, 0, half, lambda i: 2 * (i[1] ^ (1 + i[0])) + i[0]),
        (beside_too, 0, half, lambda i: 2 * (i[1] ^ (2 - i[0])) + 1 - i[0]),
        (below, 0, half, lambda i: 2 * (i[1] ^ (2 - i[0])) + i[0]),
        (below_too, 0, half, lambda i: 2 * (i[1] ^ (1 + i[0])) + 1 - i[0]),
        (across, 0, half, lambda i: 2 * (i[1] ^ 3) + i[0]),
        (across_too, 0, half, lambda i: 2 * (i[1] ^ 3) + 1 - i[0]),
    ]
    cots = [
        (first_mine, 0, quarter, lambda i: 2 * odd(i) + i[0]),
        (first_theirs, 0, quarter, lambda i: 2 * odd(i) + 1 - i[0]),
        (second_mine, 0, quarter, lambda i: 2 * (1 - odd(i)) + i[0]),
        (second_theirs, 0, quarter, lambda i: 2 * (1 - odd(i)) + 1 - i[0]),
    ]
    whole = [(cotangent, 0, width, lambda i: 0)]

    begun, own_rows = lax.cond(
        is_first,
        lambda: (
            product(info, here, slot, 0, tiles, jnp.float32),
            unset((count, units), low),
        ),
        lambda: (unset((everyone, units), jnp.float32), product(info, whole, slot, 0, tiles, low)),
    )
    one = lax.cond(
        is_first,
        lambda: product(info, rest, slot, 0, most, low, start=begun),
        lambda: product(info, here + rest, up_weight, most, few, low, room=most),
    )
    one_passed = moved(one, other_section)
    two = lax.cond(
        is_first,
        lambda: product(info, here + rest, up_weight, 0, most, low),
        lambda: product(info, cots, slot, 0, most, low, head=own_rows),
    )
    two_passed = moved(two, other_section)
    three = lax.cond(
        is_first,
        lambda: product(info, rest, slot, most, few, low, start=begun),
        lambda: product(info, cots, slot, most, few, low, head=own_rows),
    )
    three_passed = moved(three, other_section)

    every = slice(0, everyone)

    def token_part(into, at):
        options = [
            (
                lambda i, row=row: row(i) == at(i),
                array,
                lambda i, begin=begin: pl.ds(begin, half),
            )
            for array, begin, _, row in here + rest
        ]
        return (every, slice(into, into + half), options)

    def cotangent_parts():
        own = (lambda i: True, cotangent, lambda i: pl.ds(pl.multiple_of(i[2] * quarter, quarter), quarter))
        others = [
            (lambda i, row=row: row(i) == i[2], array, lambda i: pl.ds(0, quarter))
            for array, _, _, row in cots
        ]
        return [
            (slice(0, count), slice(0, quarter), [own]),
            (slice(count, everyone), slice(0, quarter), others),
        ]

    gate_slot = [token_part(0, lambda i: 2 * i[2]), token_part(half, lambda i: 2 * i[2] + 1)]
    gate_up = [token_part(0, lambda i: i[2])]
    down_slot = cotangent_parts()
    down_up = [token_part(0, lambda i: groups + i[2])]

    grads = lax.cond(
        is_first,
        lambda: outputs(
            info, True, gate_slot, gate_up, one, two_passed, two, 0, units, None
        ),
        lambda: outputs(
            info, False, down_slot, down_up, one_passed, two, two_passed, 0, units, None
        ),
    )
    slot_sum, up_sum = lax.cond(
        is_first,
        lambda: outputs(
            info, True, gate_slot, gate_up, three, three_passed, one_passed, most, units, grads
        ),
        lambda: outputs(
            info, False, down_slot, down_up, three_passed, three, one, most, units, grads
        ),
    )
    return (slot_sum[None], up_sum)


def solution(mesh):
    placed = (P("dp", "tensor"), P("section", None, "tensor"), P(None, "tensor"), P("dp", None))
    by_chip = mesh.shape["tensor"] == 4 and mesh.shape["dp"] == 4 and mesh.shape["section"] == 2

    def body(*arrays):
        return (local_by_chip if by_chip else local_plain)(mesh, *arrays)

    return jax.shard_map(
        body,
        mesh=mesh,
        in_specs=placed,
        out_specs=(P("section", "dp", "tensor"), P(("section", "dp"), "tensor")),
        check_vma=False,
    )
```

```python
import jax
import jax.numpy as jnp
from jax import lax
from jax.experimental import pallas as pl
from jax.experimental.pallas import tpu as pltpu
from jax.sharding import PartitionSpec as P


AXES = ("section", "tensor", "dp")
TILE = 512


def sent(value, mesh, target):
    shape = [mesh.shape[axis] for axis in AXES]
    pairs = []
    for s in range(shape[0]):
        for t in range(shape[1]):
            for d in range(shape[2]):
                source = (s * shape[1] + t) * shape[2] + d
                to = target(s, t, d)
                pairs.append((source, (to[0] * shape[1] + to[1]) * shape[2] + to[2]))
    return lax.ppermute(value, AXES, pairs)


def matmul(left, right):
    return jnp.dot(left, right, preferred_element_type=jnp.float32)


def along_rows(left, right):
    return lax.dot_general(
        left, right, (((0,), (0,)), ((), ())), preferred_element_type=jnp.float32
    )


def columns(value, start, width):
    return lax.dynamic_slice_in_dim(value, start, width, 1)


def gradients(gate_pre, up_pre, grad_hidden, is_first):
    sigmoid_gate = jax.nn.sigmoid(gate_pre)
    silu = gate_pre * sigmoid_gate
    grad_gate = grad_hidden * up_pre * sigmoid_gate * (1.0 + gate_pre * (1.0 - sigmoid_gate))
    right = jnp.where(is_first, grad_gate, silu * up_pre)
    return right.astype(jnp.bfloat16), (grad_hidden * silu).astype(jnp.bfloat16)


def local_plain(mesh, tokens, section_weights, up_weight, cotangent):
    section = lax.axis_index("section")
    group = lax.axis_index("dp")
    groups = mesh.shape["dp"]
    is_first = section == 0
    slot = section_weights[0]
    units = slot.shape[1]
    width = cotangent.shape[1]

    def swapped(value):
        return sent(value, mesh, lambda s, t, d: (1 - s, t, d))

    tokens_all = lax.all_gather(tokens, "tensor", axis=1, tiled=True)
    tokens_all = lax.all_gather(tokens_all, "dp", axis=0, tiled=True)
    cotangent_all = lax.all_gather(cotangent, "dp", axis=0, tiled=True)
    used = jnp.where(is_first, tokens_all, cotangent_all)
    own = matmul(used, slot).astype(jnp.bfloat16)
    other = swapped(own)
    half = units // 2
    up_own = matmul(tokens_all, columns(up_weight, section * half, half)).astype(jnp.bfloat16)
    up_other = swapped(up_own)
    up_pre = jnp.where(
        is_first,
        jnp.concatenate([up_own, up_other], 1),
        jnp.concatenate([up_other, up_own], 1),
    ).astype(jnp.float32)
    gate_pre = jnp.where(is_first, own, other).astype(jnp.float32)
    grad_hidden = jnp.where(is_first, other, own).astype(jnp.float32)
    right, grad_up = gradients(gate_pre, up_pre, grad_hidden, is_first)
    slot_rows = width // groups
    up_rows = slot_rows // 2
    slot_sum = along_rows(columns(used, group * slot_rows, slot_rows), right)
    up_sum = along_rows(columns(tokens_all, (section * groups + group) * up_rows, up_rows), grad_up)
    return (slot_sum.astype(jnp.bfloat16)[None], up_sum.astype(jnp.bfloat16))


def cost(flops, moved):
    return pl.CostEstimate(flops=int(flops), bytes_accessed=int(moved), transcendentals=0)


def product(info, pieces, weight, first_tile, tiles, dtype, start=None, head=None, room=None, parts=None):
    joined = parts or ([], [])
    flat = [(n, part) for n in (0, 1) for part in joined[n]]
    sources = []
    for _, (_, _, options) in flat:
        for _, array, _ in options:
            if not any(array is known for known in sources):
                sources.append(array)
    arrays = []
    for array, _, _, _ in pieces:
        if not any(array is a for a in arrays):
            arrays.append(array)
    which = [next(i for i, a in enumerate(arrays) if a is array) for array, _, _, _ in pieces]
    count = arrays[0].shape[0]
    above = 0 if head is None else head.shape[0]
    extras = [x for x in (start, head) if x is not None]

    def kernel(info_ref, *refs):
        lefts = refs[: len(arrays)]
        rights = refs[len(arrays) : len(arrays) + len(pieces)]
        rest = list(refs[len(arrays) + len(pieces) :])
        arrived = rest.pop() if parts else None
        targets = rest[-2:] if parts else []
        out = rest[-3] if parts else rest[-1]
        held = rest[len(extras) : len(extras) + len(sources)]

        def copies():
            for k, (n, (rows, cols, options)) in enumerate(flat):
                for when, array, taken in options:
                    ref = next(r for r, known in zip(held, sources) if known is array)
                    source = ref.at[:, taken(info_ref)]
                    target = targets[n].at[rows, cols]
                    yield when, pltpu.make_async_copy(source, target, arrived.at[k])

        if parts:

            @pl.when(pl.program_id(0) == 0)
            def _():
                for when, copy in copies():
                    pl.when(when(info_ref))(copy.start)

        total = None
        for (_, begin, depth, _), i, right in zip(pieces, which, rights):
            term = matmul(lefts[i][:, begin : begin + depth], right[...])
            total = term if total is None else total + term
        if start is not None:
            total = total + rest.pop(0)[...].astype(jnp.float32)
        if head is not None:
            out[:above, :] = rest.pop(0)[...]
        out[above:, :] = total.astype(dtype)
        if parts:

            @pl.when(pl.program_id(0) == tiles - 1)
            def _():
                for when, copy in copies():
                    pl.when(when(info_ref))(copy.wait)

    specs = [pl.BlockSpec(a.shape, lambda j, info: (0, 0)) for a in arrays]
    for _, _, depth, row in pieces:
        specs.append(
            pl.BlockSpec((depth, TILE), lambda j, info, row=row: (row(info), first_tile + j))
        )
    operands = list(arrays) + [weight] * len(pieces)
    for extra in (start, head):
        if extra is not None:
            specs.append(pl.BlockSpec((extra.shape[0], TILE), lambda j, info: (0, j)))
            operands.append(extra)
    specs += [pl.BlockSpec(memory_space=pl.ANY)] * len(sources)
    operands += sources
    out = jax.ShapeDtypeStruct((above + count, (room or tiles) * TILE), dtype)
    out_spec = pl.BlockSpec((above + count, TILE), lambda j, info: (0, j))
    outs, out_specs, scratch = out, out_spec, []
    if parts:
        shapes = [
            (max(q[0].stop for q in side), max(q[1].stop for q in side)) for side in joined
        ]
        outs = [out] + [jax.ShapeDtypeStruct(shape, jnp.bfloat16) for shape in shapes]
        out_specs = [out_spec] + [pl.BlockSpec(shape, lambda j, info: (0, 0)) for shape in shapes]
        scratch = [pltpu.SemaphoreType.DMA((len(flat),))]
    deep = sum(p[2] for p in pieces)
    return pl.pallas_call(
        kernel,
        grid_spec=pltpu.PrefetchScalarGridSpec(
            num_scalar_prefetch=1,
            grid=(tiles,),
            in_specs=specs,
            out_specs=out_specs,
            scratch_shapes=scratch,
        ),
        out_shape=outs,
        compiler_params=pltpu.CompilerParams(vmem_limit_bytes=48 * 1024 * 1024),
        cost_estimate=cost(2 * count * deep * tiles * TILE, 2 * deep * tiles * TILE + out.size * 2),
    )(info, *operands)


def unset(shape, dtype):
    return pl.pallas_call(
        lambda out: None,
        out_shape=jax.ShapeDtypeStruct(shape, dtype),
        out_specs=pl.BlockSpec(memory_space=pl.ANY),
    )()


def picked(info, blocks):
    def kernel(info_ref, *refs):
        for source, out in zip(refs[: len(blocks)], refs[len(blocks) :]):
            out[...] = source[...]

    shapes = [(array.shape[0], wide) for array, wide, _ in blocks]
    return pl.pallas_call(
        kernel,
        grid_spec=pltpu.PrefetchScalarGridSpec(
            num_scalar_prefetch=1,
            grid=(1,),
            in_specs=[
                pl.BlockSpec(shape, lambda j, info, which=which: (0, which(info)))
                for shape, (_, _, which) in zip(shapes, blocks)
            ],
            out_specs=[pl.BlockSpec(shape, lambda j, info: (0, 0)) for shape in shapes],
        ),
        out_shape=[
            jax.ShapeDtypeStruct(shape, array.dtype) for shape, (array, _, _) in zip(shapes, blocks)
        ],
    )(info, *[array for array, _, _ in blocks])


def stacked(arrays):
    count, wide = arrays[0].shape

    def kernel(*refs):
        for k, source in enumerate(refs[:-1]):
            refs[-1][k * count : (k + 1) * count, :] = source[...]

    return pl.pallas_call(
        kernel,
        out_shape=jax.ShapeDtypeStruct((len(arrays) * count, wide), arrays[0].dtype),
    )(*arrays)


def outputs(info, is_gate, left_slot, left_up, gate, hidden, up_pre, first, units, begun):
    tiles = gate.shape[1] // TILE
    count = gate.shape[0]

    def kernel(info_ref, gate_ref, hidden_ref, up_pre_ref, slot_left, up_left, *refs):
        slot_ref, up_ref = refs[-2:]
        gate_pre = gate_ref[...].astype(jnp.float32)
        grad_hidden = hidden_ref[...].astype(jnp.float32)
        up_pre = up_pre_ref[...].astype(jnp.float32)
        sigmoid_gate = jax.nn.sigmoid(gate_pre)
        silu = gate_pre * sigmoid_gate
        grad_up = (grad_hidden * silu).astype(jnp.bfloat16)
        if is_gate:
            right = grad_hidden * up_pre * sigmoid_gate * (1.0 + gate_pre * (1.0 - sigmoid_gate))
        else:
            right = silu * up_pre
        slot_ref[...] = along_rows(slot_left[...], right.astype(jnp.bfloat16)).astype(jnp.bfloat16)
        up_ref[...] = along_rows(up_left[...], grad_up).astype(jnp.bfloat16)

    here = lambda j, info: (0, j)
    there = lambda j, info: (0, j + first)
    block = (count, TILE)
    specs = [pl.BlockSpec(block, here)] * 3
    specs += [pl.BlockSpec(left.shape, lambda j, info: (0, 0)) for left in (left_slot, left_up)]
    operands = [gate, hidden, up_pre, left_slot, left_up]
    rows = (left_slot.shape[1], left_up.shape[1])
    aliases = {}
    if begun is not None:
        specs += [pl.BlockSpec(memory_space=pl.ANY)] * 2
        aliases = {1 + len(operands): 0, 2 + len(operands): 1}
        operands += list(begun)
    return pl.pallas_call(
        kernel,
        grid_spec=pltpu.PrefetchScalarGridSpec(
            num_scalar_prefetch=1,
            grid=(tiles,),
            in_specs=specs,
            out_specs=[pl.BlockSpec((r, TILE), there) for r in rows],
        ),
        out_shape=[jax.ShapeDtypeStruct((r, units), jnp.bfloat16) for r in rows],
        input_output_aliases=aliases,
        compiler_params=pltpu.CompilerParams(vmem_limit_bytes=48 * 1024 * 1024),
        cost_estimate=cost(
            2 * count * sum(rows) * tiles * TILE, 2 * tiles * TILE * (3 * count + sum(rows))
        ),
    )(info, *operands)


def local_by_chip(mesh, tokens, section_weights, up_weight, cotangent):
    groups = mesh.shape["dp"]
    section = lax.axis_index("section")
    tensor = lax.axis_index("tensor")
    group = lax.axis_index("dp")
    is_first = section == 0
    place = lax.broadcasted_iota(jnp.int32, (3,), 0)
    info = jnp.where(place == 0, section, jnp.where(place == 1, tensor, group)).astype(jnp.int32)
    slot = section_weights[0]
    count, block = tokens.shape
    half = block // 2
    width, units = slot.shape
    quarter = width // 4
    everyone = groups * count
    tiles = units // TILE
    most = (tiles + 1) // 2
    few = tiles - most
    low = jnp.bfloat16

    def moved(value, target):
        return sent(value, mesh, target)

    def ring(step):
        return lambda s, t, d: (s, t, (d + step) % groups)

    def other_section(s, t, d):
        return (1 - s, t, d)

    def near(s, t, d):
        return (s, t ^ (1 + s), d)

    def far(s, t, d):
        return (s, t ^ (2 - s), d)

    steps = range(1, groups)

    def odd(i):
        return (i[1] ^ (i[1] >> 1)) & 1

    own_half, own_quarter = picked(
        info,
        [(tokens, half, lambda i: i[0]), (cotangent, quarter, lambda i: 2 * odd(i) + i[0])],
    )

    mine = jnp.concatenate([own_half] + [moved(own_half, ring(k)) for k in steps], 0)
    theirs = moved(mine, other_section)
    first_mine = stacked([moved(own_quarter, ring(k)) for k in steps])
    beside = moved(mine, near)
    beside_too = moved(beside, other_section)
    below = moved(mine, far)
    below_too = moved(below, other_section)
    across = moved(beside, far)
    across_too = moved(across, other_section)
    first_theirs = moved(first_mine, other_section)
    second_mine = moved(first_mine, near)
    second_theirs = moved(second_mine, other_section)

    here = [
        (mine, 0, half, lambda i: 2 * i[1] + i[0]),
        (theirs, 0, half, lambda i: 2 * i[1] + 1 - i[0]),
    ]
    rest = [
        (beside, 0, half, lambda i: 2 * (i[1] ^ (1 + i[0])) + i[0]),
        (beside_too, 0, half, lambda i: 2 * (i[1] ^ (2 - i[0])) + 1 - i[0]),
        (below, 0, half, lambda i: 2 * (i[1] ^ (2 - i[0])) + i[0]),
        (below_too, 0, half, lambda i: 2 * (i[1] ^ (1 + i[0])) + 1 - i[0]),
        (across, 0, half, lambda i: 2 * (i[1] ^ 3) + i[0]),
        (across_too, 0, half, lambda i: 2 * (i[1] ^ 3) + 1 - i[0]),
    ]
    cots = [
        (first_mine, 0, quarter, lambda i: 2 * odd(i) + i[0]),
        (first_theirs, 0, quarter, lambda i: 2 * odd(i) + 1 - i[0]),
        (second_mine, 0, quarter, lambda i: 2 * (1 - odd(i)) + i[0]),
        (second_theirs, 0, quarter, lambda i: 2 * (1 - odd(i)) + 1 - i[0]),
    ]
    whole = [(cotangent, 0, width, lambda i: 0)]

    def own_rows(begin, many):
        return product(info, whole, slot, begin, many, low)

    own_high = lax.cond(
        is_first,
        lambda: unset((count, few * TILE), low),
        lambda: own_rows(most, few),
    )
    begun, own_low = lax.cond(
        is_first,
        lambda: (product(info, here, slot, 0, most, jnp.float32), unset((count, most * TILE), low)),
        lambda: (unset((everyone, most * TILE), jnp.float32), own_rows(0, most)),
    )
    one = lax.cond(
        is_first,
        lambda: product(info, rest, slot, 0, most, low, start=begun),
        lambda: product(info, here + rest, up_weight, most, few, low, room=most),
    )
    one_passed = moved(one, other_section)
    two = lax.cond(
        is_first,
        lambda: product(info, here + rest, up_weight, 0, most, low),
        lambda: product(info, cots, slot, 0, most, low, head=own_low),
    )
    two_passed = moved(two, other_section)
    every = slice(0, everyone)

    def token_part(into, at):
        options = [
            (
                lambda i, row=row: row(i) == at(i),
                array,
                lambda i, begin=begin: pl.ds(begin, half),
            )
            for array, begin, _, row in here + rest
        ]
        return (every, slice(into, into + half), options)

    def cotangent_parts():
        own = (lambda i: True, cotangent, lambda i: pl.ds(pl.multiple_of(i[2] * quarter, quarter), quarter))
        others = [
            (lambda i, row=row: row(i) == i[2], array, lambda i: pl.ds(0, quarter))
            for array, _, _, row in cots
        ]
        return [
            (slice(0, count), slice(0, quarter), [own]),
            (slice(count, everyone), slice(0, quarter), others),
        ]

    gate_slot = [token_part(0, lambda i: 2 * i[2]), token_part(half, lambda i: 2 * i[2] + 1)]
    gate_up = [token_part(0, lambda i: i[2])]
    down_slot = cotangent_parts()
    down_up = [token_part(0, lambda i: groups + i[2])]

    three, left_slot, left_up = lax.cond(
        is_first,
        lambda: tuple(
            product(
                info, here + rest, slot, most, few, low, parts=(gate_slot, gate_up)
            )
        ),
        lambda: tuple(
            product(
                info, cots, slot, most, few, low, head=own_high, parts=(down_slot, down_up)
            )
        ),
    )
    three_passed = moved(three, other_section)

    grads = lax.cond(
        is_first,
        lambda: outputs(
            info, True, left_slot, left_up, one, two_passed, two, 0, units, None
        ),
        lambda: outputs(
            info, False, left_slot, left_up, one_passed, two, two_passed, 0, units, None
        ),
    )
    slot_sum, up_sum = lax.cond(
        is_first,
        lambda: outputs(
            info, True, left_slot, left_up, three, three_passed, one_passed, most, units, grads
        ),
        lambda: outputs(
            info, False, left_slot, left_up, three_passed, three, one, most, units, grads
        ),
    )
    return (slot_sum[None], up_sum)


def solution(mesh):
    placed = (P("dp", "tensor"), P("section", None, "tensor"), P(None, "tensor"), P("dp", None))
    by_chip = mesh.shape["tensor"] == 4 and mesh.shape["dp"] == 4 and mesh.shape["section"] == 2

    def body(*arrays):
        return (local_by_chip if by_chip else local_plain)(mesh, *arrays)

    return jax.shard_map(
        body,
        mesh=mesh,
        in_specs=placed,
        out_specs=(P("section", "dp", "tensor"), P(("section", "dp"), "tensor")),
        check_vma=False,
    )
```

```python
import jax
import jax.numpy as jnp
from jax import lax
from jax.experimental import pallas as pl
from jax.experimental.pallas import tpu as pltpu
from jax.sharding import PartitionSpec as P


AXES = ("section", "tensor", "dp")
TILE = 512


def sent(value, mesh, target):
    shape = [mesh.shape[axis] for axis in AXES]
    pairs = []
    for s in range(shape[0]):
        for t in range(shape[1]):
            for d in range(shape[2]):
                source = (s * shape[1] + t) * shape[2] + d
                to = target(s, t, d)
                pairs.append((source, (to[0] * shape[1] + to[1]) * shape[2] + to[2]))
    return lax.ppermute(value, AXES, pairs)


def matmul(left, right):
    return jnp.dot(left, right, preferred_element_type=jnp.float32)


def along_rows(left, right):
    return lax.dot_general(
        left, right, (((0,), (0,)), ((), ())), preferred_element_type=jnp.float32
    )


def columns(value, start, width):
    return lax.dynamic_slice_in_dim(value, start, width, 1)


def gradients(gate_pre, up_pre, grad_hidden, is_first):
    sigmoid_gate = jax.nn.sigmoid(gate_pre)
    silu = gate_pre * sigmoid_gate
    grad_gate = grad_hidden * up_pre * sigmoid_gate * (1.0 + gate_pre * (1.0 - sigmoid_gate))
    right = jnp.where(is_first, grad_gate, silu * up_pre)
    return right.astype(jnp.bfloat16), (grad_hidden * silu).astype(jnp.bfloat16)


def local_plain(mesh, tokens, section_weights, up_weight, cotangent):
    section = lax.axis_index("section")
    group = lax.axis_index("dp")
    groups = mesh.shape["dp"]
    is_first = section == 0
    slot = section_weights[0]
    units = slot.shape[1]
    width = cotangent.shape[1]

    def swapped(value):
        return sent(value, mesh, lambda s, t, d: (1 - s, t, d))

    tokens_all = lax.all_gather(tokens, "tensor", axis=1, tiled=True)
    tokens_all = lax.all_gather(tokens_all, "dp", axis=0, tiled=True)
    cotangent_all = lax.all_gather(cotangent, "dp", axis=0, tiled=True)
    used = jnp.where(is_first, tokens_all, cotangent_all)
    own = matmul(used, slot).astype(jnp.bfloat16)
    other = swapped(own)
    half = units // 2
    up_own = matmul(tokens_all, columns(up_weight, section * half, half)).astype(jnp.bfloat16)
    up_other = swapped(up_own)
    up_pre = jnp.where(
        is_first,
        jnp.concatenate([up_own, up_other], 1),
        jnp.concatenate([up_other, up_own], 1),
    ).astype(jnp.float32)
    gate_pre = jnp.where(is_first, own, other).astype(jnp.float32)
    grad_hidden = jnp.where(is_first, other, own).astype(jnp.float32)
    right, grad_up = gradients(gate_pre, up_pre, grad_hidden, is_first)
    slot_rows = width // groups
    up_rows = slot_rows // 2
    slot_sum = along_rows(columns(used, group * slot_rows, slot_rows), right)
    up_sum = along_rows(columns(tokens_all, (section * groups + group) * up_rows, up_rows), grad_up)
    return (slot_sum.astype(jnp.bfloat16)[None], up_sum.astype(jnp.bfloat16))


def cost(flops, moved):
    return pl.CostEstimate(flops=int(flops), bytes_accessed=int(moved), transcendentals=0)


def product(info, pieces, weight, first_tile, tiles, dtype, start=None, head=None, room=None, parts=None):
    joined = parts or ([], [])
    flat = [(n, part) for n in (0, 1) for part in joined[n]]
    sources = []
    for _, (_, _, options) in flat:
        for _, array, _ in options:
            if not any(array is known for known in sources):
                sources.append(array)
    arrays = []
    for array, _, _, _ in pieces:
        if not any(array is a for a in arrays):
            arrays.append(array)
    which = [next(i for i, a in enumerate(arrays) if a is array) for array, _, _, _ in pieces]
    count = arrays[0].shape[0]
    above = 0 if head is None else head.shape[0]
    extras = [x for x in (start, head) if x is not None]

    def kernel(info_ref, *refs):
        lefts = refs[: len(arrays)]
        rights = refs[len(arrays) : len(arrays) + len(pieces)]
        rest = list(refs[len(arrays) + len(pieces) :])
        arrived = rest.pop() if parts else None
        targets = rest[-2:] if parts else []
        out = rest[-3] if parts else rest[-1]
        held = rest[len(extras) : len(extras) + len(sources)]

        def copies():
            for k, (n, (rows, cols, options)) in enumerate(flat):
                for when, array, taken in options:
                    ref = next(r for r, known in zip(held, sources) if known is array)
                    source = ref.at[:, taken(info_ref)]
                    target = targets[n].at[rows, cols]
                    yield when, pltpu.make_async_copy(source, target, arrived.at[k])

        if parts:

            @pl.when(pl.program_id(0) == 0)
            def _():
                for when, copy in copies():
                    pl.when(when(info_ref))(copy.start)

        total = None
        for (_, begin, depth, _), i, right in zip(pieces, which, rights):
            term = matmul(lefts[i][:, begin : begin + depth], right[...])
            total = term if total is None else total + term
        if start is not None:
            total = total + rest.pop(0)[...].astype(jnp.float32)
        if head is not None:
            out[:above, :] = rest.pop(0)[...]
        out[above:, :] = total.astype(dtype)
        if parts:

            @pl.when(pl.program_id(0) == tiles - 1)
            def _():
                for when, copy in copies():
                    pl.when(when(info_ref))(copy.wait)

    specs = [pl.BlockSpec(a.shape, lambda j, info: (0, 0)) for a in arrays]
    for _, _, depth, row in pieces:
        specs.append(
            pl.BlockSpec((depth, TILE), lambda j, info, row=row: (row(info), first_tile + j))
        )
    operands = list(arrays) + [weight] * len(pieces)
    for extra in (start, head):
        if extra is not None:
            specs.append(pl.BlockSpec((extra.shape[0], TILE), lambda j, info: (0, j)))
            operands.append(extra)
    specs += [pl.BlockSpec(memory_space=pl.ANY)] * len(sources)
    operands += sources
    out = jax.ShapeDtypeStruct((above + count, (room or tiles) * TILE), dtype)
    out_spec = pl.BlockSpec((above + count, TILE), lambda j, info: (0, j))
    outs, out_specs, scratch = out, out_spec, []
    if parts:
        shapes = [
            (max(q[0].stop for q in side), max(q[1].stop for q in side)) for side in joined
        ]
        outs = [out] + [jax.ShapeDtypeStruct(shape, jnp.bfloat16) for shape in shapes]
        out_specs = [out_spec] + [pl.BlockSpec(shape, lambda j, info: (0, 0)) for shape in shapes]
        scratch = [pltpu.SemaphoreType.DMA((len(flat),))]
    deep = sum(p[2] for p in pieces)
    return pl.pallas_call(
        kernel,
        grid_spec=pltpu.PrefetchScalarGridSpec(
            num_scalar_prefetch=1,
            grid=(tiles,),
            in_specs=specs,
            out_specs=out_specs,
            scratch_shapes=scratch,
        ),
        out_shape=outs,
        compiler_params=pltpu.CompilerParams(vmem_limit_bytes=48 * 1024 * 1024),
        cost_estimate=cost(2 * count * deep * tiles * TILE, 2 * deep * tiles * TILE + out.size * 2),
    )(info, *operands)


def unset(shape, dtype):
    return pl.pallas_call(
        lambda out: None,
        out_shape=jax.ShapeDtypeStruct(shape, dtype),
        out_specs=pl.BlockSpec(memory_space=pl.ANY),
    )()


def picked(info, blocks):
    def kernel(info_ref, *refs):
        for source, out in zip(refs[: len(blocks)], refs[len(blocks) :]):
            out[...] = source[...]

    shapes = [(array.shape[0], wide) for array, wide, _ in blocks]
    return pl.pallas_call(
        kernel,
        grid_spec=pltpu.PrefetchScalarGridSpec(
            num_scalar_prefetch=1,
            grid=(1,),
            in_specs=[
                pl.BlockSpec(shape, lambda j, info, which=which: (0, which(info)))
                for shape, (_, _, which) in zip(shapes, blocks)
            ],
            out_specs=[pl.BlockSpec(shape, lambda j, info: (0, 0)) for shape in shapes],
        ),
        out_shape=[
            jax.ShapeDtypeStruct(shape, array.dtype) for shape, (array, _, _) in zip(shapes, blocks)
        ],
    )(info, *[array for array, _, _ in blocks])


def stacked(arrays):
    count, wide = arrays[0].shape

    def kernel(*refs):
        for k, source in enumerate(refs[:-1]):
            refs[-1][k * count : (k + 1) * count, :] = source[...]

    return pl.pallas_call(
        kernel,
        out_shape=jax.ShapeDtypeStruct((len(arrays) * count, wide), arrays[0].dtype),
    )(*arrays)


def outputs(info, is_gate, left_slot, left_up, gate, hidden, up_pre, first, units, begun):
    tiles = gate.shape[1] // TILE
    count = gate.shape[0]

    def kernel(info_ref, gate_ref, hidden_ref, up_pre_ref, slot_left, up_left, *refs):
        slot_ref, up_ref = refs[-2:]
        gate_pre = gate_ref[...].astype(jnp.float32)
        grad_hidden = hidden_ref[...].astype(jnp.float32)
        up_pre = up_pre_ref[...].astype(jnp.float32)
        sigmoid_gate = jax.nn.sigmoid(gate_pre)
        silu = gate_pre * sigmoid_gate
        grad_up = (grad_hidden * silu).astype(jnp.bfloat16)
        if is_gate:
            right = grad_hidden * up_pre * sigmoid_gate * (1.0 + gate_pre * (1.0 - sigmoid_gate))
        else:
            right = silu * up_pre
        slot_ref[...] = along_rows(slot_left[...], right.astype(jnp.bfloat16)).astype(jnp.bfloat16)
        up_ref[...] = along_rows(up_left[...], grad_up).astype(jnp.bfloat16)

    here = lambda j, info: (0, j)
    there = lambda j, info: (0, j + first)
    block = (count, TILE)
    specs = [pl.BlockSpec(block, here)] * 3
    specs += [pl.BlockSpec(left.shape, lambda j, info: (0, 0)) for left in (left_slot, left_up)]
    operands = [gate, hidden, up_pre, left_slot, left_up]
    rows = (left_slot.shape[1], left_up.shape[1])
    aliases = {}
    if begun is not None:
        specs += [pl.BlockSpec(memory_space=pl.ANY)] * 2
        aliases = {1 + len(operands): 0, 2 + len(operands): 1}
        operands += list(begun)
    return pl.pallas_call(
        kernel,
        grid_spec=pltpu.PrefetchScalarGridSpec(
            num_scalar_prefetch=1,
            grid=(tiles,),
            in_specs=specs,
            out_specs=[pl.BlockSpec((r, TILE), there) for r in rows],
        ),
        out_shape=[jax.ShapeDtypeStruct((r, units), jnp.bfloat16) for r in rows],
        input_output_aliases=aliases,
        compiler_params=pltpu.CompilerParams(vmem_limit_bytes=48 * 1024 * 1024),
        cost_estimate=cost(
            2 * count * sum(rows) * tiles * TILE, 2 * tiles * TILE * (3 * count + sum(rows))
        ),
    )(info, *operands)


def local_by_chip(mesh, tokens, section_weights, up_weight, cotangent):
    groups = mesh.shape["dp"]
    section = lax.axis_index("section")
    tensor = lax.axis_index("tensor")
    group = lax.axis_index("dp")
    is_first = section == 0
    place = lax.broadcasted_iota(jnp.int32, (3,), 0)
    info = jnp.where(place == 0, section, jnp.where(place == 1, tensor, group)).astype(jnp.int32)
    slot = section_weights[0]
    count, block = tokens.shape
    half = block // 2
    width, units = slot.shape
    quarter = width // 4
    everyone = groups * count
    tiles = units // TILE
    most = (tiles + 1) // 2
    few = tiles - most
    low = jnp.bfloat16

    def moved(value, target):
        return sent(value, mesh, target)

    def ring(step):
        return lambda s, t, d: (s, t, (d + step) % groups)

    def other_section(s, t, d):
        return (1 - s, t, d)

    def near(s, t, d):
        return (s, t ^ (1 + s), d)

    def far(s, t, d):
        return (s, t ^ (2 - s), d)

    steps = range(1, groups)

    def odd(i):
        return (i[1] ^ (i[1] >> 1)) & 1

    own_half, own_quarter = picked(
        info,
        [(tokens, half, lambda i: i[0]), (cotangent, quarter, lambda i: 2 * odd(i) + i[0])],
    )

    mine = jnp.concatenate([own_half] + [moved(own_half, ring(k)) for k in steps], 0)
    theirs = moved(mine, other_section)
    first_mine = stacked([moved(own_quarter, ring(k)) for k in steps])
    beside = moved(mine, near)
    beside_too = moved(beside, other_section)
    below = moved(mine, far)
    below_too = moved(below, other_section)
    across = moved(beside, far)
    across_too = moved(across, other_section)
    first_theirs = moved(first_mine, other_section)
    second_mine = moved(first_mine, near)
    second_theirs = moved(second_mine, other_section)

    here = [
        (mine, 0, half, lambda i: 2 * i[1] + i[0]),
        (theirs, 0, half, lambda i: 2 * i[1] + 1 - i[0]),
    ]
    rest = [
        (beside, 0, half, lambda i: 2 * (i[1] ^ (1 + i[0])) + i[0]),
        (beside_too, 0, half, lambda i: 2 * (i[1] ^ (2 - i[0])) + 1 - i[0]),
        (below, 0, half, lambda i: 2 * (i[1] ^ (2 - i[0])) + i[0]),
        (below_too, 0, half, lambda i: 2 * (i[1] ^ (1 + i[0])) + 1 - i[0]),
        (across, 0, half, lambda i: 2 * (i[1] ^ 3) + i[0]),
        (across_too, 0, half, lambda i: 2 * (i[1] ^ 3) + 1 - i[0]),
    ]
    cots = [
        (first_mine, 0, quarter, lambda i: 2 * odd(i) + i[0]),
        (first_theirs, 0, quarter, lambda i: 2 * odd(i) + 1 - i[0]),
        (second_mine, 0, quarter, lambda i: 2 * (1 - odd(i)) + i[0]),
        (second_theirs, 0, quarter, lambda i: 2 * (1 - odd(i)) + 1 - i[0]),
    ]
    whole = [(cotangent, 0, width, lambda i: 0)]

    def own_rows(begin, many):
        return product(info, whole, slot, begin, many, low)

    own_high = lax.cond(
        is_first,
        lambda: unset((count, few * TILE), low),
        lambda: own_rows(most, few),
    )
    begun, own_low = lax.cond(
        is_first,
        lambda: (
            product(info, here, slot, 0, most, low),
            unset((count, most * TILE), low),
        ),
        lambda: (unset((everyone, most * TILE), low), own_rows(0, most)),
    )
    one = lax.cond(
        is_first,
        lambda: product(info, rest, slot, 0, most, low, start=begun),
        lambda: product(info, here + rest, up_weight, most, few, low, room=most),
    )
    one_passed = moved(one, other_section)
    two = lax.cond(
        is_first,
        lambda: product(info, here + rest, up_weight, 0, most, low),
        lambda: product(info, cots, slot, 0, most, low, head=own_low),
    )
    two_passed = moved(two, other_section)
    every = slice(0, everyone)

    def token_part(into, at):
        options = [
            (
                lambda i, row=row: row(i) == at(i),
                array,
                lambda i, begin=begin: pl.ds(begin, half),
            )
            for array, begin, _, row in here + rest
        ]
        return (every, slice(into, into + half), options)

    def cotangent_parts():
        own = (lambda i: True, cotangent, lambda i: pl.ds(pl.multiple_of(i[2] * quarter, quarter), quarter))
        others = [
            (lambda i, row=row: row(i) == i[2], array, lambda i: pl.ds(0, quarter))
            for array, _, _, row in cots
        ]
        return [
            (slice(0, count), slice(0, quarter), [own]),
            (slice(count, everyone), slice(0, quarter), others),
        ]

    gate_slot = [token_part(0, lambda i: 2 * i[2]), token_part(half, lambda i: 2 * i[2] + 1)]
    gate_up = [token_part(0, lambda i: i[2])]
    down_slot = cotangent_parts()
    down_up = [token_part(0, lambda i: groups + i[2])]

    three, left_slot, left_up = lax.cond(
        is_first,
        lambda: tuple(
            product(
                info, here + rest, slot, most, few, low, parts=(gate_slot, gate_up)
            )
        ),
        lambda: tuple(
            product(
                info, cots, slot, most, few, low, head=own_high, parts=(down_slot, down_up)
            )
        ),
    )
    three_passed = moved(three, other_section)

    grads = lax.cond(
        is_first,
        lambda: outputs(
            info, True, left_slot, left_up, one, two_passed, two, 0, units, None
        ),
        lambda: outputs(
            info, False, left_slot, left_up, one_passed, two, two_passed, 0, units, None
        ),
    )
    slot_sum, up_sum = lax.cond(
        is_first,
        lambda: outputs(
            info, True, left_slot, left_up, three, three_passed, one_passed, most, units, grads
        ),
        lambda: outputs(
            info, False, left_slot, left_up, three_passed, three, one, most, units, grads
        ),
    )
    return (slot_sum[None], up_sum)


def solution(mesh):
    placed = (P("dp", "tensor"), P("section", None, "tensor"), P(None, "tensor"), P("dp", None))
    by_chip = mesh.shape["tensor"] == 4 and mesh.shape["dp"] == 4 and mesh.shape["section"] == 2

    def body(*arrays):
        return (local_by_chip if by_chip else local_plain)(mesh, *arrays)

    return jax.shard_map(
        body,
        mesh=mesh,
        in_specs=placed,
        out_specs=(P("section", "dp", "tensor"), P(("section", "dp"), "tensor")),
        check_vma=False,
    )
```
